32 devices in a mesh: brick: 16 (over z, y, core), view: 2 (over x).
Axes of the slice: x: 2, y: 2, z: 4, core: 2. Of those that a mesh axis runs over, the one named last changes fastest.
Arguments:
- estimate: float32 [256, 128, 128], P('brick', 'view'), may hold values from 0.5 to 2
- views_data: float32 [2, 256, 128, 128], P('view', 'brick'), may hold values from 0.5 to 2
- psf_taps: float32 [2, 3, 17], P('view'), may hold values from 0.05 to 1
- view_offsets: int32 [2, 2], P('view'), may hold values from -4 to 4
- coverage: int32 [16, 2], P('brick'), may hold values from 0 to 1, as said below
Outputs:
- deconvolved: float32 [256, 128, 128], P('brick', 'view')
The draws below stay inside these ranges and needn't reach their ends.
Inputs may be any that keep to these rules, and one draw needn't show every extreme that they name: `coverage`: every slab is covered by at least one view.
All inputs are finite; a program needn't handle non-finite values.
Results may differ from the reference program's by a relative error of at most 0.0001.
Values sent between devices are 32-bit elements; how exact they have to be, the bound alone decides.
No kernel may reach another device: no remote copies, remote signals or barrier semaphores. Data moves between devices by JAX's collectives and lax.ppermute only.
A program may use at most 64 MiB of HBM per device.

```python
import math
import jax
import jax.numpy as jnp
from jax import lax

SZ = 16
NY = 128
NX = 128
R = 8
ITERS = 4
KW = 17
VIEWS = 2
BRICKS = 16
NZ = 256


def draw_coverage(key, part):
    first_key = jax.random.fold_in(key, 11)
    second_key = jax.random.fold_in(key, 23)
    levels = jax.random.randint(first_key, (BRICKS, VIEWS), 0, 4)
    chosen = jax.random.randint(second_key, (BRICKS, 1), 0, VIEWS)
    onehot = jnp.arange(VIEWS, dtype=jnp.int32)[None, :] == chosen
    return jnp.where((levels > 0) | onehot, 1, 0).astype(jnp.int32)


def plant(array, key, smallest, high):
    longest = array.shape.index(max(array.shape))
    spots = []
    for shift in (0, 1):
        where = [jax.random.randint(jax.random.fold_in(key, axis), (), 0, length) for axis, length in enumerate(array.shape)]
        where[longest] = (where[longest] + shift) % array.shape[longest]
        spots.append(tuple(where))
    return array.at[spots[0]].set(smallest).at[spots[1]].set(high)


def shard_levels(stream_key, dims, split, least, largest):
    loudness = 1.0
    for axis_at, parts in split:
        draws = jax.random.uniform(jax.random.fold_in(jax.random.fold_in(stream_key, 6), axis_at), (parts,), jnp.float32, least / len(split), largest / len(split))
        loudness = loudness * jnp.repeat(jnp.exp(draws), dims[axis_at] // parts).reshape((-1,) + (1,) * (len(dims) - 1 - axis_at))
    return loudness


def setup_inputs(seed: int = 0) -> dict:
    streams_of = jax.random.split(jax.random.key(seed), 6)
    estimate = jnp.clip(0.5 + 1.5 * jax.random.uniform(streams_of[0], (NZ, NY, NX), jnp.float32) ** shard_levels(streams_of[0], (NZ, NY, NX), ((0, 16), (1, 2)), -0.2, 0.2), 0.5, 2.0)
    views_data = jnp.clip(0.5 + 1.5 * jax.random.uniform(streams_of[1], (VIEWS, NZ, NY, NX), jnp.float32) ** shard_levels(streams_of[1], (VIEWS, NZ, NY, NX), ((0, 2), (1, 16)), -0.2, 0.2), 0.5, 2.0)
    psf_taps = jnp.clip(jnp.exp(math.log(1.0) - 2.9957323 * jax.random.uniform(streams_of[2], (VIEWS, 3, KW), jnp.float32) ** shard_levels(streams_of[2], (VIEWS, 3, KW), ((0, 2),), -0.2, 0.2)), 0.05, 1.0)
    view_offsets = plant(jax.random.randint(streams_of[3], (VIEWS, 2), 0 - R // 2, R // 2 + 1), jax.random.fold_in(streams_of[3], 1), 0 - R // 2, (R // 2 + 1) - 1).astype(jnp.int32)
    coverage = draw_coverage(jax.random.fold_in(streams_of[5], 71), 0)
    return {"estimate": estimate, "views_data": views_data, "psf_taps": psf_taps, "view_offsets": view_offsets, "coverage": coverage}


high = lax.Precision.HIGHEST


def make_band(row, offset, count):
    rows_at = jnp.arange(count, dtype=jnp.int32)[:, None]
    cols_at = jnp.arange(count, dtype=jnp.int32)[None, :]
    index = cols_at - rows_at + offset + R
    taps_at = jnp.arange(row.shape[0], dtype=jnp.int32)
    onehot = index[:, :, None] == taps_at[None, None, :]
    return jnp.sum(jnp.where(onehot, row[None, None, :], 0.0), axis=-1)


def along_first(volume, taps_row, mirror):
    padded = jnp.pad(volume, ((R, R), (0, 0), (0, 0)))
    total = jnp.zeros_like(volume)
    for k in range(2 * R + 1):
        start = 2 * R - k if mirror else k
        total = total + taps_row[k] * padded[start:start + volume.shape[0]]
    return total


def reference(estimate, views_data, psf_taps, view_offsets, coverage):
    taps = psf_taps / jnp.sum(psf_taps, axis=-1, keepdims=True)
    cover_cells = jnp.repeat(coverage.astype(jnp.float32), SZ, axis=0)
    count_cells = jnp.sum(cover_cells, axis=1)[:, None, None]
    current = estimate
    for step in range(ITERS):
        def one_view(view, total):
            row = taps[view]
            band_y = make_band(row[1], view_offsets[view, 0], NY)
            band_x = make_band(row[2], view_offsets[view, 1], NX)
            blurred = along_first(current, row[0], False)
            blurred = jnp.einsum('ij,zjx->zix', band_y, blurred, precision=high)
            blurred = jnp.einsum('zyj,ij->zyi', blurred, band_x, precision=high)
            ratio = views_data[view] / blurred
            back = jnp.einsum('zyi,ij->zyj', ratio, band_x, precision=high)
            back = jnp.einsum('ij,zix->zjx', band_y, back, precision=high)
            back = along_first(back, row[0], True)
            flag = lax.dynamic_index_in_dim(cover_cells, view, 1, keepdims=False)
            return total + flag[:, None, None] * jnp.log(back)
        merged = lax.fori_loop(0, VIEWS, one_view, jnp.zeros_like(current))
        current = current * jnp.exp(merged / count_cells)
    return current
```

```python
import jax
import jax.numpy as jnp
from jax import lax
from jax.sharding import PartitionSpec as P

R = 8
ITERS = 4
HALO = 2 * R


def pair_lists(count):
    inner = [(i, i + 1) for i in range(0, count - 1, 2)]
    outer = [(i, i + 1) for i in range(1, count - 1, 2)]
    both = lambda pairs: [p for a, b in pairs for p in ((a, b), (b, a))]
    return both(inner), both(outer)


def diagonal(pairs):
    return [(2 * a + v, 2 * b + 1 - v) for a, b in pairs for v in range(2)]


def near(block, at_end, depth, dim=0):
    start = jnp.where(at_end, block.shape[dim] - depth, 0)
    return lax.dynamic_slice_in_dim(block, start, depth, axis=dim)


def bands(rows, shift, rows_at, cols_at):
    index = cols_at[None, :] - rows_at[:, None] + shift[:, None, None] + R
    taps_at = jnp.arange(rows.shape[-1], dtype=jnp.int32)
    onehot = index[..., None] == taps_at
    return jnp.sum(jnp.where(onehot, rows[:, None, None, :], 0.0), axis=-1)


def two_view_plan(estimate, views_data, psf_taps, view_offsets, coverage):
    brick, view = lax.axis_index("brick"), lax.axis_index("view")
    inner, outer = pair_lists(lax.axis_size("brick"))
    swap = [(0, 1), (1, 0)]
    even = lax.rem(brick, 2) == 0
    first = view == 0
    rows = estimate.shape[1]
    total = views_data.shape[2]

    small = jnp.concatenate(
        [psf_taps[0].reshape(-1), view_offsets[0].astype(jnp.float32)]
    )
    both = jnp.stack([small, lax.ppermute(small, "view", swap)])
    kernels = both[:, : psf_taps[0].size].reshape((2,) + psf_taps.shape[1:])
    shifts = jnp.round(both[:, psf_taps[0].size :]).astype(jnp.int32)
    cover = coverage[0].astype(jnp.float32)
    cover = jnp.where(first, cover, cover[::-1])

    recorded = views_data[0]

    def window(at):
        own = lax.dynamic_slice_in_dim(recorded, at * rows, rows, axis=1)
        start = jnp.where(at == 0, rows, total - rows - HALO)
        return jnp.concatenate(
            [own, lax.dynamic_slice_in_dim(recorded, start, HALO, axis=1)], axis=1
        )

    mine, theirs = window(view), window(1 - view)
    other = lax.ppermute(theirs, "view", swap)
    data = jnp.stack(
        [
            jnp.concatenate(
                [
                    mine,
                    lax.ppermute(near(mine, even, R), "brick", inner),
                    lax.ppermute(near(mine, ~even, R), "brick", outer),
                ],
                axis=0,
            ),
            jnp.concatenate(
                [
                    other,
                    lax.ppermute(near(other, even, R), "brick", inner),
                    lax.ppermute(near(theirs, ~even, R), ("brick", "view"), diagonal(outer)),
                ],
                axis=0,
            ),
        ]
    )

    def halo(current):
        edge = near(current, first, HALO, 1)
        side = lax.ppermute(edge, "view", swap)
        inner_z = lax.ppermute(current, "brick", inner)
        outer_z = lax.ppermute(current, "brick", outer)
        outer_side = lax.ppermute(edge, ("brick", "view"), diagonal(outer))
        inner_side = lax.ppermute(side, "brick", inner)
        return (current, side), (inner_z, inner_side), (outer_z, outer_side)

    own_rows = jnp.arange(rows, dtype=jnp.int32)
    side_rows = jnp.arange(HALO, dtype=jnp.int32) + jnp.where(first, rows, -HALO)
    rows_at = jnp.concatenate([own_rows, side_rows])
    return kernels, shifts, cover, data, halo, rows_at


def many_view_plan(estimate, views_data, psf_taps, view_offsets, coverage):
    even = lax.rem(lax.axis_index("brick"), 2) == 0
    inner, outer = pair_lists(lax.axis_size("brick"))
    up = [(i, i + 1) for i in range(lax.axis_size("view") - 1)]
    down = [(b, a) for a, b in up]
    rows = estimate.shape[1]

    def side_rows(block, dim):
        low = lax.slice_in_dim(block, rows - HALO, rows, axis=dim)
        high = lax.slice_in_dim(block, 0, HALO, axis=dim)
        return jnp.concatenate(
            [lax.ppermute(low, "view", up), lax.ppermute(high, "view", down)], axis=dim
        )

    kernels = lax.all_gather(psf_taps, "view", axis=0, tiled=True)
    shifts = lax.all_gather(view_offsets, "view", axis=0, tiled=True)
    cover = coverage[0].astype(jnp.float32)
    data = lax.all_to_all(views_data, "view", split_axis=2, concat_axis=0, tiled=True)
    data = jnp.concatenate(
        [
            data,
            lax.ppermute(near(data, even, R, 1), "brick", inner),
            lax.ppermute(near(data, ~even, R, 1), "brick", outer),
        ],
        axis=1,
    )
    data = jnp.concatenate([data, side_rows(data, 2)], axis=2)

    def halo(current):
        blocks = (
            current,
            lax.ppermute(current, "brick", inner),
            lax.ppermute(current, "brick", outer),
        )
        return tuple((block, side_rows(block, 1)) for block in blocks)

    own_rows = jnp.arange(rows, dtype=jnp.int32)
    edge_rows = jnp.arange(HALO, dtype=jnp.int32)
    rows_at = jnp.concatenate([own_rows, edge_rows - HALO, edge_rows + rows])
    return kernels, shifts, cover, data, halo, rows_at


def shards(estimate, views_data, psf_taps, view_offsets, coverage):
    depth, rows, width = estimate.shape
    plan = two_view_plan if lax.axis_size("view") == 2 else many_view_plan
    kernels, shifts, cover, data, halo, rows_at = plan(
        estimate, views_data, psf_taps, view_offsets, coverage
    )
    taps = kernels / jnp.sum(kernels, axis=-1, keepdims=True)
    even = lax.rem(lax.axis_index("brick"), 2) == 0
    layers = jnp.arange(depth, dtype=jnp.int32)
    after = jnp.arange(HALO, dtype=jnp.int32) + depth
    before = jnp.arange(HALO, dtype=jnp.int32) - HALO
    in_at = jnp.concatenate([layers, jnp.where(even, after, before), jnp.where(even, before, after)])
    ratio_at = jnp.concatenate(
        [
            layers,
            jnp.where(even, after[:R], before[-R:]),
            jnp.where(even, before[-R:], after[:R]),
        ]
    )
    cols_at = jnp.arange(width, dtype=jnp.int32)
    none = jnp.zeros_like(shifts[:, 0])
    z_band = bands(taps[:, 0], none, ratio_at, in_at)
    z_back = jnp.swapaxes(bands(taps[:, 0], none, ratio_at, layers), 1, 2)
    y_band = bands(taps[:, 1], shifts[:, 0], rows_at, rows_at)
    y_back = jnp.swapaxes(y_band[:, :, :rows], 1, 2)
    x_band = bands(taps[:, 2], shifts[:, 1], cols_at, cols_at)
    count = jnp.sum(cover)
    dot = lambda spec, a, b: jnp.einsum(spec, a, b, precision=lax.Precision.HIGH)
    current = estimate
    for step in range(ITERS):
        pieces = halo(current)
        whole = jnp.concatenate([jnp.concatenate(p, axis=1) for p in pieces], axis=0)
        blurred = dot("vij,zjx->vzix", y_band, whole)
        blurred = dot("vzyj,vij->vzyi", blurred, x_band)
        blurred = dot("vip,vpyx->viyx", z_band, blurred)
        ratio = jnp.where(blurred > 0, data / blurred, 0.0)
        back = dot("vip,vpyx->viyx", z_back, ratio)
        back = dot("vzyi,vij->vzyj", back, x_band)
        back = dot("vji,vzix->vzjx", y_back, back)
        merged = sum(cover[v] * jnp.log(back[v]) for v in range(back.shape[0]))
        current = current * jnp.exp(merged / count)
    return current


def solution(mesh):
    return jax.shard_map(
        shards,
        mesh=mesh,
        in_specs=(
            P("brick", "view", None),
            P("view", "brick", None, None),
            P("view", None, None),
            P("view", None),
            P("brick", None),
        ),
        out_specs=P("brick", "view", None),
        check_vma=False,
    )
```

```python
import functools
import jax
import jax.numpy as jnp
from jax import lax
from jax.experimental import pallas as pl
from jax.experimental.pallas import tpu as pltpu
from jax.sharding import PartitionSpec as P

R = 8
ITERS = 4
HALO = 2 * R
F32, BF16 = jnp.float32, jnp.bfloat16
VMEM = pl.BlockSpec(memory_space=pltpu.VMEM)
SMEM = pl.BlockSpec(memory_space=pltpu.SMEM)


def parts(x):
    top = x.astype(BF16)
    return top, (x - top.astype(F32)).astype(BF16)


def dot(a, b):
    return jnp.dot(a, b, preferred_element_type=F32)


def stack3(blocks):
    split = [parts(b) for b in blocks]
    tops, rests = [s[0] for s in split], [s[1] for s in split]
    return jnp.concatenate(tops + rests + tops, axis=0)


def blur_rows_and_columns(own, side, ly, bx, mid, out, flip):
    depth, rows, width = own.shape
    views, window = bx.shape[0], rows + side.shape[1]
    for z in range(0, depth, 2):
        pair = stack3([jnp.concatenate([ref[z], ref[z + 1]], axis=1) for ref in (own, side)])
        result = dot(ly[...], pair)
        for v in range(views):
            for i in range(2):
                top, rest = parts(result[v * window : (v + 1) * window, i * width : (i + 1) * width])
                at = pl.ds((z + i) * window, window)
                mid[v, at, :width] = top
                mid[v, at, width:] = rest
    for v in range(views):
        for z in range(0, depth, 4):
            wide = dot(mid[v, pl.ds(z * window, 4 * window), :], bx[v])
            value = wide[:, :width] + wide[:, width:]
            for i in range(4):
                to = depth - 1 - z - i if flip else z + i
                out[v, to] = value[i * window : (i + 1) * window]


def tap(taps, v, k, even):
    return taps[v, lax.select(even, jnp.int32(k), jnp.int32(2 * R - k))]


def half_ratio(first, second, data, taps, v, y, even, depth):
    at = pl.ds(y, R)
    load = lambda i: first[v, i, at, :] if i < depth else second[v, i - depth, at, :]
    blurred = [None] * depth
    for k in range(2 * R + 1):
        t = tap(taps, v, k, even)
        for j in range(depth):
            term = t * load(j + k)
            blurred[j] = term if blurred[j] is None else blurred[j] + term
    return [
        jnp.where(blurred[j] > 0, data[v, j, at, :] / blurred[j], 0.0) for j in range(depth)
    ]


def near_kernel(taps, parity, own, side, own_in, side_in, data, ly, bx, blur_own, back, blur_in, mid):
    depth = own.shape[0]
    views, window = bx.shape[0], ly.shape[1] // 3
    even = parity[0] == 0
    blur_rows_and_columns(own, side, ly, bx, mid, blur_own, False)
    blur_rows_and_columns(own_in, side_in, ly, bx, mid, blur_in, True)
    for v in range(views):

        @pl.loop(0, window // R)
        def _(tile):
            y = pl.multiple_of(tile * R, R)
            ratio = half_ratio(blur_own, blur_in, data, taps, v, y, even, depth)
            total = [None] * depth
            for d in range(depth):
                t = tap(taps, v, d, even)
                for j in range(depth - d):
                    term = t * ratio[j]
                    total[j + d] = term if total[j + d] is None else total[j + d] + term
            for z in range(depth):
                back[v, z, pl.ds(y, R), :] = total[z]


def far_kernel(last, taps, parity, weight, own_out, side_out, data, blur_own, back, est, ly, bx, lyt, bxt, *rest):
    if last:
        out, blur_out, full, mid = rest
    else:
        out, edge, blur_out, full, mid = rest
    depth, rows, width = est.shape
    views, window = bx.shape[0], ly.shape[1] // 3
    even = parity[0] == 0
    blur_rows_and_columns(own_out, side_out, ly, bx, mid, blur_out, True)
    for v in range(views):

        @pl.loop(0, window // R)
        def _(tile):
            y = pl.multiple_of(tile * R, R)
            ratio = half_ratio(blur_out, blur_own, data, taps, v, y, even, depth)
            total = [back[v, z, pl.ds(y, R), :] for z in range(depth)]
            for d in range(depth):
                t = tap(taps, v, 2 * R - d, even)
                for z in range(depth - d):
                    total[z] = total[z] + t * ratio[z + d]
            for z in range(depth):
                full[v, z, pl.ds(y, R), :] = total[z]

    for z in range(0, depth, 2):
        for v in range(views):
            result = dot(lyt[v], stack3([jnp.concatenate([full[v, z], full[v, z + 1]], axis=1)]))
            for i in range(2):
                top, rest_ = parts(result[:, i * width : (i + 1) * width])
                at = pl.ds((z + i) * rows, rows)
                mid[v, at, :width] = top
                mid[v, at, width:] = rest_
    for z in range(0, depth, 4):
        factor = None
        total = None
        for v in range(views):
            wide = dot(mid[v, pl.ds(z * rows, 4 * rows), :], bxt[v])
            value = wide[:, :width] + wide[:, width:]
            w = weight[v]
            if views == 2:
                power = jnp.where(w == 1.0, value, jnp.where(w == 0.0, 1.0, jnp.sqrt(value)))
                factor = power if factor is None else factor * power
            else:
                term = w * jnp.log(value)
                total = term if total is None else total + term
        if factor is None:
            factor = jnp.exp(total)
        for i in range(4):
            new = est[z + i] * factor[i * rows : (i + 1) * rows]
            if last:
                out[lax.select(even, jnp.int32(z + i), jnp.int32(depth - 1 - z - i))] = new
            else:
                out[z + i] = new
                edge[z + i] = jnp.where(parity[1] == 0, new[rows - HALO :], new[:HALO])


def near(taps, parity, own, side, own_in, side_in, data, ly, bx):
    depth, rows, width = own.shape
    views, window = bx.shape[0], rows + side.shape[1]
    shape = (views, depth, window, width)
    size = views * depth * window * width
    return pl.pallas_call(
        near_kernel,
        out_shape=[jax.ShapeDtypeStruct(shape, F32)] * 2,
        in_specs=[SMEM] * 2 + [VMEM] * 7,
        out_specs=[VMEM] * 2,
        scratch_shapes=[pltpu.VMEM(shape, F32), pltpu.VMEM((views, depth * window, 2 * width), BF16)],
        compiler_params=pltpu.CompilerParams(vmem_limit_bytes=(24 if views == 2 else 48) << 20),
        cost_estimate=pl.CostEstimate(flops=size * 4000, bytes_accessed=size * 16, transcendentals=0),
        name="near",
    )(taps, parity, own, side, own_in, side_in, data, ly, bx)


def far(last, taps, parity, weight, own_out, side_out, data, blur_own, back, est, ly, bx, lyt, bxt):
    depth, rows, width = est.shape
    views, window = bx.shape[0], rows + side_out.shape[1]
    shape = (views, depth, window, width)
    size = views * depth * window * width
    outs = [jax.ShapeDtypeStruct(est.shape, F32)]
    if not last:
        outs.append(jax.ShapeDtypeStruct((depth, HALO, width), F32))
    return pl.pallas_call(
        functools.partial(far_kernel, last),
        out_shape=outs,
        in_specs=[SMEM] * 3 + [VMEM] * 10,
        out_specs=[VMEM] * len(outs),
        scratch_shapes=[pltpu.VMEM(shape, F32)] * 2 + [pltpu.VMEM((views, depth * window, 2 * width), BF16)],
        compiler_params=pltpu.CompilerParams(vmem_limit_bytes=(24 if views == 2 else 48) << 20),
        cost_estimate=pl.CostEstimate(flops=size * 4000, bytes_accessed=size * 16, transcendentals=0),
        name="far",
    )(taps, parity, weight, own_out, side_out, data, blur_own, back, est, ly, bx, lyt, bxt)


def band_kernel(taps, shifts, place, ly, lyt, bx, bxt):
    views, rows, triple = lyt.shape
    window, width = triple // 3, bx.shape[1] // 2
    low = place[2]
    iota = lambda shape, dim: lax.broadcasted_iota(jnp.int32, shape, dim)

    def position(c):
        return jnp.where(c < rows, c, jnp.where(c < rows + low, c - rows - HALO, c - low))

    def values(v, d, index):
        total = jnp.zeros(index.shape, F32)
        for k in range(2 * R + 1):
            total = jnp.where(index == k, taps[v, d * (2 * R + 1) + k], total)
        return total

    def split(value):
        top = value.astype(BF16).astype(F32)
        return top, value - top

    for v in range(views):
        for out, height, mirror in ((ly, window, False), (lyt, rows, True)):
            col = iota((height, triple), 1)
            folded = position(
                jnp.where(col < window, col, jnp.where(col < 2 * window, col - window, col - 2 * window))
            )
            line = position(iota((height, triple), 0))
            index = (line - folded if mirror else folded - line) + shifts[v, 0] + R
            top, rest = split(values(v, 1, index))
            both = jnp.where(col < 2 * window, top, rest).astype(BF16)
            if mirror:
                out[v] = both
            else:
                out[pl.ds(v * window, window), :] = both
        step = iota((width, width), 1) - iota((width, width), 0)
        for out, index in ((bx, -step), (bxt, step)):
            top, rest = split(values(v, 2, index + shifts[v, 1] + R))
            for i in range(2):
                at = pl.ds(i * width, width)
                out[v, at, :width] = top.astype(BF16)
                out[v, at, width:] = rest.astype(BF16)


def make_bands(taps, shifts, place, rows, window, width):
    views = taps.shape[0]
    shapes = [
        (views * window, 3 * window),
        (views, rows, 3 * window),
        (views, 2 * width, 2 * width),
        (views, 2 * width, 2 * width),
    ]
    return pl.pallas_call(
        band_kernel,
        out_shape=[jax.ShapeDtypeStruct(s, BF16) for s in shapes],
        in_specs=[SMEM] * 3,
        out_specs=[VMEM] * 4,
        compiler_params=pltpu.CompilerParams(vmem_limit_bytes=8 << 20),
        cost_estimate=pl.CostEstimate(flops=views * 10**8, bytes_accessed=views * 10**6, transcendentals=0),
        name="bands",
    )(taps, shifts, place)


def pair_lists(count):
    inner = [(i, i + 1) for i in range(0, count - 1, 2)]
    outer = [(i, i + 1) for i in range(1, count - 1, 2)]
    both = lambda pairs: [p for a, b in pairs for p in ((a, b), (b, a))]
    return both(inner), both(outer)


def diagonal(pairs):
    return [(2 * a + v, 2 * b + 1 - v) for a, b in pairs for v in range(2)]


def facing(block, even):
    return jnp.where(even, block, block[::-1])


def two_view_plan(estimate, views_data, taps, view_offsets, even, inner, outer):
    first = lax.axis_index("view") == 0
    swap = [(0, 1), (1, 0)]
    rows, total = estimate.shape[1], views_data.shape[2]

    def halo(current, edge):
        side = lax.ppermute(edge, "view", swap)
        outer_z = lax.ppermute(current, "brick", outer)
        outer_side = lax.ppermute(edge, ("brick", "view"), diagonal(outer))
        inner_z = lax.ppermute(current, "brick", inner)
        inner_side = lax.ppermute(side, "brick", inner)
        return side, inner_z, inner_side, outer_z, outer_side

    current = facing(estimate, even)
    edge = lax.dynamic_slice_in_dim(current, jnp.where(first, rows - HALO, 0), HALO, axis=1)

    small = jnp.concatenate([taps[0], view_offsets[0].astype(F32)])
    both = jnp.stack([small, lax.ppermute(small, "view", swap)])
    all_taps = both[:, : taps.shape[1]]
    shifts = jnp.round(both[:, taps.shape[1] :]).astype(jnp.int32)

    recorded = views_data[0]

    def window(at):
        own = lax.dynamic_slice_in_dim(recorded, at * rows, rows, axis=1)
        start = jnp.where(at == 0, rows, total - rows - HALO)
        beside = lax.dynamic_slice_in_dim(recorded, start, HALO, axis=1)
        return facing(jnp.concatenate([own, beside], axis=1), even)

    view = lax.axis_index("view")
    mine, theirs = window(view), window(1 - view)
    other = lax.ppermute(theirs, "view", swap)
    mine_far = lax.ppermute(mine[:R], "brick", outer)
    other_far = lax.ppermute(theirs[:R], ("brick", "view"), diagonal(outer))
    mine_near = lax.ppermute(mine[-R:], "brick", inner)
    other_near = lax.ppermute(other[-R:], "brick", inner)
    near_data = jnp.stack(
        [
            jnp.concatenate([mine[-R:], mine_near[::-1]]),
            jnp.concatenate([other[-R:], other_near[::-1]]),
        ]
    )
    far_data = jnp.stack(
        [
            jnp.concatenate([mine_far[::-1], mine[:R]]),
            jnp.concatenate([other_far[::-1], other[:R]]),
        ]
    )
    low = jnp.where(first, 0, HALO)
    return current, edge, all_taps, shifts, near_data, far_data, halo, low, rows + HALO


def many_view_plan(estimate, views_data, taps, view_offsets, even, inner, outer):
    rows = estimate.shape[1]
    up = [(i, i + 1) for i in range(lax.axis_size("view") - 1)]
    down = [(b, a) for a, b in up]

    def beside(block, dim):
        low = lax.slice_in_dim(block, rows - HALO, rows, axis=dim)
        high = lax.slice_in_dim(block, 0, HALO, axis=dim)
        return jnp.concatenate(
            [lax.ppermute(low, "view", up), lax.ppermute(high, "view", down)], axis=dim
        )

    def halo(current, _):
        inner_z = lax.ppermute(current, "brick", inner)
        outer_z = lax.ppermute(current, "brick", outer)
        return beside(current, 1), inner_z, beside(inner_z, 1), outer_z, beside(outer_z, 1)

    all_taps = lax.all_gather(taps, "view", axis=0, tiled=True)
    shifts = lax.all_gather(view_offsets, "view", axis=0, tiled=True)
    data = lax.all_to_all(views_data, "view", split_axis=2, concat_axis=0, tiled=True)
    data = jnp.where(even, data, data[:, ::-1])
    data = jnp.concatenate([data, beside(data, 2)], axis=2)
    inner_data = lax.ppermute(data[:, -R:], "brick", inner)[:, ::-1]
    outer_data = lax.ppermute(data[:, :R], "brick", outer)[:, ::-1]
    near_data = jnp.concatenate([data[:, -R:], inner_data], axis=1)
    far_data = jnp.concatenate([outer_data, data[:, :R]], axis=1)
    current = facing(estimate, even)
    return current, None, all_taps, shifts, near_data, far_data, halo, HALO, rows + 2 * HALO


def shards(estimate, views_data, psf_taps, view_offsets, coverage):
    brick, view = lax.axis_index("brick"), lax.axis_index("view")
    depth, rows, width = estimate.shape
    inner, outer = pair_lists(lax.axis_size("brick"))
    even = lax.rem(brick, 2) == 0
    taps = psf_taps / jnp.sum(psf_taps, axis=-1, keepdims=True)
    taps = taps.reshape(1, -1)
    pair = lax.axis_size("view") == 2
    plan = two_view_plan if pair else many_view_plan
    current, edge, taps, shifts, near_data, far_data, halo, low, window = plan(
        estimate, views_data, taps, view_offsets, even, inner, outer
    )
    cover = coverage[0].astype(F32)
    if pair:
        cover = jnp.where(view == 0, cover, cover[::-1])
    weight = cover / jnp.sum(cover)
    place = jnp.stack([lax.rem(brick, 2), view, low]).astype(jnp.int32)
    ly, lyt, bx, bxt = make_bands(taps, shifts, place, rows, window, width)
    for step in range(ITERS):
        last = step == ITERS - 1
        side, inner_z, inner_side, outer_z, outer_side = halo(current, edge)
        blur_own, back = near(
            taps, place, current, side, inner_z, inner_side, near_data, ly, bx
        )
        results = far(
            last, taps, place, weight, outer_z, outer_side, far_data, blur_own, back, current, ly, bx, lyt, bxt
        )
        current = results[0]
        edge = None if last else results[1]
    return current


def solution(mesh):
    return jax.shard_map(
        shards,
        mesh=mesh,
        in_specs=(
            P("brick", "view", None),
            P("view", "brick", None, None),
            P("view", None, None),
            P("view", None),
            P("brick", None),
        ),
        out_specs=P("brick", "view", None),
        check_vma=False,
    )
```

```python
import functools
import jax
import jax.numpy as jnp
from jax import lax
from jax.experimental import pallas as pl
from jax.experimental.pallas import tpu as pltpu
from jax.sharding import PartitionSpec as P


R = 8
ITERS = 4
HALO = 2 * R

F32, BF16 = jnp.float32, jnp.bfloat16
VMEM = pl.BlockSpec(memory_space=pltpu.VMEM)
SMEM = pl.BlockSpec(memory_space=pltpu.SMEM)


def parts(x):
    top = x.astype(BF16)
    return top, (x - top.astype(F32)).astype(BF16)


def dot(a, b):
    return jnp.dot(a, b, preferred_element_type=F32)


def stack3(blocks):
    split = [parts(b) for b in blocks]
    tops, rests = [s[0] for s in split], [s[1] for s in split]
    return jnp.concatenate(tops + rests + tops, axis=0)


def blur_rows_and_columns(own, side, ly, bx, mid, out, flip):
    depth, rows, width = own.shape
    views, window = bx.shape[0], rows + side.shape[1]
    for z in range(0, depth, 2):
        pair = stack3([jnp.concatenate([ref[z], ref[z + 1]], axis=1) for ref in (own, side)])
        result = dot(ly[...], pair)
        for v in range(views):
            for i in range(2):
                top, rest = parts(result[v * window : (v + 1) * window, i * width : (i + 1) * width])
                at = pl.ds((z + i) * window, window)
                mid[v, at, :width] = top
                mid[v, at, width:] = rest
    for v in range(views):
        for z in range(0, depth, 4):
            wide = dot(mid[v, pl.ds(z * window, 4 * window), :], bx[v])
            value = wide[:, :width] + wide[:, width:]
            for i in range(4):
                to = depth - 1 - z - i if flip else z + i
                out[v, to] = value[i * window : (i + 1) * window]


def tap(taps, v, k, even):
    return taps[v, lax.select(even, jnp.int32(k), jnp.int32(2 * R - k))]


def ratios(seen, blurred):
    return [jnp.where(b > 0, d / b, 0.0) for d, b in zip(seen, blurred)]


def gather(total, at, term):
    total[at] = term if total[at] is None else total[at] + term


def near_kernel(views, taps, parity, own, side, own_in, side_in, ly, bx, *refs):
    data_own, data_in = refs[:views], refs[views : 2 * views]
    blur_far, back, blur_own, blur_in, mid = refs[2 * views :]
    depth = own.shape[0]
    window = ly.shape[1] // 3
    even = parity[0] == 0
    blur_rows_and_columns(own, side, ly, bx, mid, blur_own, False)
    blur_rows_and_columns(own_in, side_in, ly, bx, mid, blur_in, True)
    for v in range(views):

        @pl.loop(0, window // R)
        def _(tile):
            at = pl.ds(pl.multiple_of(tile * R, R), R)
            load = lambda i: blur_own[v, i, at, :] if i < depth else blur_in[v, i - depth, at, :]
            blurred = [None] * depth
            for k in range(2 * R + 1):
                t = tap(taps, v, k, even)
                for j in range(depth):
                    gather(blurred, j, t * load(j + k))
            seen = [data_own[v][j, at, :] for j in range(R)]
            seen += [data_in[v][R - 1 - j, at, :] for j in range(R)]
            ratio = ratios(seen, blurred)
            total = [None] * depth
            for d in range(depth):
                t = tap(taps, v, d, even)
                for j in range(depth - d):
                    gather(total, j + d, t * ratio[j])
            for z in range(depth):
                back[v, z, at, :] = total[z]
            partial = [None] * depth
            for k in range(1, 2 * R + 1):
                t = tap(taps, v, k, even)
                for j in range(max(0, depth - k), depth):
                    gather(partial, j, t * load(j + k - depth))
            for j in range(depth):
                blur_far[v, j, at, :] = (
                    jnp.zeros_like(total[0]) if partial[j] is None else partial[j]
                )


def far_kernel(last, views, taps, parity, weight, own_out, side_out, blur_far, back, est, ly, bx, lyt, bxt, *refs):
    data_out, data_own = refs[:views], refs[views : 2 * views]
    out, edge = refs[2 * views], None if last else refs[2 * views + 1]
    blur_out, full, mid = refs[-3:]
    depth, rows, width = est.shape
    window = ly.shape[1] // 3
    even = parity[0] == 0
    blur_rows_and_columns(own_out, side_out, ly, bx, mid, blur_out, True)
    for v in range(views):

        @pl.loop(0, window // R)
        def _(tile):
            at = pl.ds(pl.multiple_of(tile * R, R), R)
            blurred = [blur_far[v, j, at, :] for j in range(depth)]
            for k in range(2 * R):
                t = tap(taps, v, k, even)
                for j in range(depth - k):
                    blurred[j] = blurred[j] + t * blur_out[v, j + k, at, :]
            seen = [data_out[v][R - 1 - j, at, :] for j in range(R)]
            seen += [data_own[v][j, at, :] for j in range(R)]
            ratio = ratios(seen, blurred)
            total = [back[v, z, at, :] for z in range(depth)]
            for d in range(depth):
                t = tap(taps, v, 2 * R - d, even)
                for z in range(depth - d):
                    total[z] = total[z] + t * ratio[z + d]
            for z in range(depth):
                full[v, z, at, :] = total[z]

    for z in range(0, depth, 2):
        for v in range(views):
            result = dot(lyt[v], stack3([jnp.concatenate([full[v, z], full[v, z + 1]], axis=1)]))
            for i in range(2):
                top, rest = parts(result[:, i * width : (i + 1) * width])
                at = pl.ds((z + i) * rows, rows)
                mid[v, at, :width] = top
                mid[v, at, width:] = rest
    for z in range(0, depth, 4):
        factor = None
        total = None
        for v in range(views):
            wide = dot(mid[v, pl.ds(z * rows, 4 * rows), :], bxt[v])
            value = wide[:, :width] + wide[:, width:]
            w = weight[v]
            if views == 2:
                power = jnp.where(w == 1.0, value, jnp.where(w == 0.0, 1.0, jnp.sqrt(value)))
                factor = power if factor is None else factor * power
            else:
                term = w * jnp.log(value)
                total = term if total is None else total + term
        if factor is None:
            factor = jnp.exp(total)
        for i in range(4):
            new = est[z + i] * factor[i * rows : (i + 1) * rows]
            if last:
                out[lax.select(even, jnp.int32(z + i), jnp.int32(depth - 1 - z - i))] = new
            else:
                out[z + i] = new
                edge[z + i] = jnp.where(parity[1] == 0, new[rows - HALO :], new[:HALO])


def near(taps, place, own, side, own_in, side_in, ly, bx, data_own, data_in):
    depth, rows, width = own.shape
    views, window = bx.shape[0], rows + side.shape[1]
    shape = (views, depth, window, width)
    size = views * depth * window * width
    return pl.pallas_call(
        functools.partial(near_kernel, views),
        out_shape=[jax.ShapeDtypeStruct(shape, F32)] * 2,
        in_specs=[SMEM] * 2 + [VMEM] * (6 + 2 * views),
        out_specs=[VMEM] * 2,
        scratch_shapes=[pltpu.VMEM(shape, F32)] * 2
        + [pltpu.VMEM((views, depth * window, 2 * width), BF16)],
        compiler_params=pltpu.CompilerParams(vmem_limit_bytes=(24 if views == 2 else 48) << 20),
        cost_estimate=pl.CostEstimate(flops=size * 4000, bytes_accessed=size * 16, transcendentals=0),
        name="near",
    )(taps, place, own, side, own_in, side_in, ly, bx, *data_own, *data_in)


def far(last, taps, place, weight, own_out, side_out, blur_far, back, est, ly, bx, lyt, bxt, data_out, data_own):
    depth, rows, width = est.shape
    views, window = bx.shape[0], rows + side_out.shape[1]
    shape = (views, depth, window, width)
    size = views * depth * window * width
    outs = [jax.ShapeDtypeStruct(est.shape, F32)]
    if not last:
        outs.append(jax.ShapeDtypeStruct((depth, HALO, width), F32))
    return pl.pallas_call(
        functools.partial(far_kernel, last, views),
        out_shape=outs,
        in_specs=[SMEM] * 3 + [VMEM] * (9 + 2 * views),
        out_specs=[VMEM] * len(outs),
        scratch_shapes=[pltpu.VMEM(shape, F32)] * 2
        + [pltpu.VMEM((views, depth * window, 2 * width), BF16)],
        compiler_params=pltpu.CompilerParams(vmem_limit_bytes=(24 if views == 2 else 48) << 20),
        cost_estimate=pl.CostEstimate(flops=size * 4000, bytes_accessed=size * 16, transcendentals=0),
        name="far",
    )(taps, place, weight, own_out, side_out, blur_far, back, est, ly, bx, lyt, bxt, *data_out, *data_own)


def estimate_kernel(place, estimate, out, edge):
    depth, rows, _ = estimate.shape
    start = pl.multiple_of(jnp.where(place[1] == 0, rows - HALO, 0), HALO)
    for z in range(depth):
        at = lax.select(place[0] == 0, jnp.int32(z), jnp.int32(depth - 1 - z))
        out[z] = estimate[at]
        edge[z] = estimate[at, pl.ds(start, HALO), :]


def recorded_kernel(place, recorded, mine_out, mine_in, theirs_out, theirs_in):
    _, depth, total, _ = recorded.shape
    rows = total // 2
    for z in range(depth):
        at = lax.select(place[0] == 0, jnp.int32(z), jnp.int32(depth - 1 - z))
        for view, outs in ((place[1], (mine_out, mine_in)), (1 - place[1], (theirs_out, theirs_in))):
            out, to = (outs[0], z) if z < depth // 2 else (outs[1], z - depth // 2)
            start = pl.multiple_of(view * rows, R)
            out[to, :rows] = recorded[0, at, pl.ds(start, rows), :]
            start = pl.multiple_of(jnp.where(view == 0, rows, total - rows - HALO), R)
            out[to, rows:] = recorded[0, at, pl.ds(start, HALO), :]


def simple_call(body, place, array, shapes):
    return pl.pallas_call(
        body,
        out_shape=[jax.ShapeDtypeStruct(shape, F32) for shape in shapes],
        in_specs=[SMEM, VMEM],
        out_specs=[VMEM] * len(shapes),
        compiler_params=pltpu.CompilerParams(vmem_limit_bytes=8 << 20),
        cost_estimate=pl.CostEstimate(flops=0, bytes_accessed=8 * array.size, transcendentals=0),
    )(place, array)


def band_kernel(taps, shifts, place, ly, lyt, bx, bxt):
    views, rows, triple = lyt.shape
    window, width = triple // 3, bx.shape[1] // 2
    low = place[2]
    iota = lambda shape, dim: lax.broadcasted_iota(jnp.int32, shape, dim)

    def position(c):
        return jnp.where(c < rows, c, jnp.where(c < rows + low, c - rows - HALO, c - low))

    def values(v, d, index):
        total = jnp.zeros(index.shape, F32)
        for k in range(2 * R + 1):
            total = jnp.where(index == k, taps[v, d * (2 * R + 1) + k], total)
        return total

    def split(value):
        top = value.astype(BF16).astype(F32)
        return top, value - top

    for v in range(views):
        for out, height, mirror in ((ly, window, False), (lyt, rows, True)):
            col = iota((height, triple), 1)
            folded = position(
                jnp.where(col < window, col, jnp.where(col < 2 * window, col - window, col - 2 * window))
            )
            line = position(iota((height, triple), 0))
            index = (line - folded if mirror else folded - line) + shifts[v, 0] + R
            top, rest = split(values(v, 1, index))
            both = jnp.where(col < 2 * window, top, rest).astype(BF16)
            if mirror:
                out[v] = both
            else:
                out[pl.ds(v * window, window), :] = both
        step = iota((width, width), 1) - iota((width, width), 0)
        for out, index in ((bx, -step), (bxt, step)):
            top, rest = split(values(v, 2, index + shifts[v, 1] + R))
            for i in range(2):
                at = pl.ds(i * width, width)
                out[v, at, :width] = top.astype(BF16)
                out[v, at, width:] = rest.astype(BF16)


def make_bands(taps, shifts, place, rows, window, width):
    views = taps.shape[0]
    shapes = [
        (views * window, 3 * window),
        (views, rows, 3 * window),
        (views, 2 * width, 2 * width),
        (views, 2 * width, 2 * width),
    ]
    return pl.pallas_call(
        band_kernel,
        out_shape=[jax.ShapeDtypeStruct(s, BF16) for s in shapes],
        in_specs=[SMEM] * 3,
        out_specs=[VMEM] * 4,
        compiler_params=pltpu.CompilerParams(vmem_limit_bytes=8 << 20),
        cost_estimate=pl.CostEstimate(flops=views * 10**8, bytes_accessed=views * 10**6, transcendentals=0),
        name="bands",
    )(taps, shifts, place)


def pair_lists(count):
    inner = [(i, i + 1) for i in range(0, count - 1, 2)]
    outer = [(i, i + 1) for i in range(1, count - 1, 2)]
    both = lambda pairs: [p for a, b in pairs for p in ((a, b), (b, a))]
    return both(inner), both(outer)


def diagonal(pairs):
    return [(2 * a + v, 2 * b + 1 - v) for a, b in pairs for v in range(2)]


def two_view_plan(estimate, views_data, taps, view_offsets, place, inner, outer):
    swap = [(0, 1), (1, 0)]
    depth, rows, width = estimate.shape
    window = rows + HALO
    axes = ("brick", "view")
    first = place[1] == 0

    def halo(current, edge):
        outer_z = lax.ppermute(current, "brick", outer)
        outer_side = lax.ppermute(edge, axes, diagonal(outer))
        side = lax.ppermute(edge, "view", swap)
        inner_z = lax.ppermute(current, "brick", inner)
        inner_side = lax.ppermute(edge, axes, diagonal(inner))
        return side, inner_z, inner_side, outer_z, outer_side

    prep = jnp.concatenate([place, jnp.where(first, 0, HALO)[None]]).astype(jnp.int32)
    current, edge = simple_call(estimate_kernel, prep, estimate, [estimate.shape, (depth, HALO, width)])
    small = jnp.concatenate([taps[0], view_offsets[0].astype(F32)])
    both = jnp.stack([small, lax.ppermute(small, "view", swap)])
    all_taps = both[:, : taps.shape[1]]
    shifts = jnp.round(both[:, taps.shape[1] :]).astype(jnp.int32)

    mine_out, mine_in, theirs_out, theirs_in = simple_call(
        recorded_kernel, prep, views_data, [(depth // 2, window, width)] * 4
    )
    other_in = lax.ppermute(theirs_in, "view", swap)
    other_out = lax.ppermute(theirs_out, "view", swap)
    mine_far = lax.ppermute(mine_out, "brick", outer)
    other_far = lax.ppermute(theirs_out, axes, diagonal(outer))
    mine_near = lax.ppermute(mine_in, "brick", inner)
    other_near = lax.ppermute(other_in, "brick", inner)
    near_data = (mine_in, other_in), (mine_near, other_near)
    far_data = (mine_far, other_far), (mine_out, other_out)
    return current, edge, all_taps, shifts, near_data, far_data, halo, prep, window


def many_view_plan(estimate, views_data, taps, view_offsets, place, inner, outer):
    rows = estimate.shape[1]
    even = place[0] == 0
    up = [(i, i + 1) for i in range(lax.axis_size("view") - 1)]
    down = [(b, a) for a, b in up]

    def beside(block, dim):
        low = lax.slice_in_dim(block, rows - HALO, rows, axis=dim)
        high = lax.slice_in_dim(block, 0, HALO, axis=dim)
        return jnp.concatenate(
            [lax.ppermute(low, "view", up), lax.ppermute(high, "view", down)], axis=dim
        )

    def halo(current, _):
        inner_z = lax.ppermute(current, "brick", inner)
        outer_z = lax.ppermute(current, "brick", outer)
        return beside(current, 1), inner_z, beside(inner_z, 1), outer_z, beside(outer_z, 1)

    all_taps = lax.all_gather(taps, "view", axis=0, tiled=True)
    shifts = lax.all_gather(view_offsets, "view", axis=0, tiled=True)
    data = lax.all_to_all(views_data, "view", split_axis=2, concat_axis=0, tiled=True)
    data = jnp.where(even, data, data[:, ::-1])
    data = jnp.concatenate([data, beside(data, 2)], axis=2)
    views = range(data.shape[0])
    ends = lambda array: tuple(array[v] for v in views)
    mine_in, mine_out = data[:, -R:], data[:, :R]
    near_data = ends(mine_in), ends(lax.ppermute(mine_in, "brick", inner))
    far_data = ends(lax.ppermute(mine_out, "brick", outer)), ends(mine_out)
    current = jnp.where(even, estimate, estimate[::-1])
    place = jnp.concatenate([place, jnp.full((1,), HALO, place.dtype)])
    return current, None, all_taps, shifts, near_data, far_data, halo, place, rows + 2 * HALO


def shards(estimate, views_data, psf_taps, view_offsets, coverage):
    brick, view = lax.axis_index("brick"), lax.axis_index("view")
    _, rows, width = estimate.shape
    inner, outer = pair_lists(lax.axis_size("brick"))
    pair = lax.axis_size("view") == 2
    plan = two_view_plan if pair else many_view_plan
    taps = psf_taps / jnp.sum(psf_taps, axis=-1, keepdims=True)
    taps = taps.reshape(1, -1)
    place = jnp.stack([lax.rem(brick, 2), view]).astype(jnp.int32)
    current, edge, taps, shifts, near_data, far_data, halo, place, window = plan(
        estimate, views_data, taps, view_offsets, place, inner, outer
    )
    cover = coverage[0].astype(F32)
    if pair:
        cover = jnp.where(view == 0, cover, cover[::-1])
    weight = cover / jnp.sum(cover)
    ly, lyt, bx, bxt = make_bands(taps, shifts, place, rows, window, width)
    for step in range(ITERS):
        last = step == ITERS - 1
        side, inner_z, inner_side, outer_z, outer_side = halo(current, edge)
        blur_far, back = near(
            taps, place, current, side, inner_z, inner_side, ly, bx, *near_data
        )
        results = far(
            last, taps, place, weight, outer_z, outer_side, blur_far, back, current, ly, bx, lyt, bxt, *far_data
        )
        current = results[0]
        edge = None if last else results[1]
    return current


def solution(mesh):
    return jax.shard_map(
        shards,
        mesh=mesh,
        in_specs=(
            P("brick", "view", None),
            P("view", "brick", None, None),
            P("view", None, None),
            P("view", None),
            P("brick", None),
        ),
        out_specs=P("brick", "view", None),
        check_vma=False,
    )
```

```python
import jax
import jax.numpy as jnp
from jax import lax
from jax.experimental import pallas as pl
from jax.experimental.pallas import tpu as pltpu
from jax.sharding import PartitionSpec as P


R = 8
ITERS = 4
HALO = 2 * R

F32, BF16 = jnp.float32, jnp.bfloat16
VMEM = pl.BlockSpec(memory_space=pltpu.VMEM)
SMEM = pl.BlockSpec(memory_space=pltpu.SMEM)
TAPS = 2 * R + 1


def parts(x):
    top = x.astype(BF16)
    return top, (x - top.astype(F32)).astype(BF16)


def dot(a, b):
    return jnp.dot(a, b, preferred_element_type=F32)


def stack3(blocks):
    split = [parts(b) for b in blocks]
    tops, rests = [s[0] for s in split], [s[1] for s in split]
    return jnp.concatenate(tops + rests + tops, axis=0)


class Piece:
    def __init__(self, array, rows, start=0):
        self.array, self.rows, self.start = array, rows, start

    def on(self, ref):
        return Piece(ref, self.rows, self.start)

    def layer(self, z):
        return self.array[pl.ds(self.start + z * self.rows, self.rows), :]

    def tile(self, z, y):
        return self.array[pl.ds(pl.multiple_of(self.start + z * self.rows + y, R), R), :]


def call(body, scalars, pieces, out_shape, scratch, vmem, cost):
    arrays = []
    for piece in pieces:
        if not any(piece.array is array for array in arrays):
            arrays.append(piece.array)
    where = [next(i for i, array in enumerate(arrays) if array is p.array) for p in pieces]

    def kernel(*refs):
        inputs = refs[len(scalars) : len(scalars) + len(arrays)]
        body(
            refs[: len(scalars)],
            [p.on(inputs[i]) for p, i in zip(pieces, where)],
            *refs[len(scalars) + len(arrays) :],
        )

    return pl.pallas_call(
        kernel,
        out_shape=out_shape,
        in_specs=[SMEM] * len(scalars) + [VMEM] * len(arrays),
        out_specs=[VMEM] * len(out_shape),
        scratch_shapes=scratch,
        compiler_params=pltpu.CompilerParams(vmem_limit_bytes=vmem << 20),
        cost_estimate=pl.CostEstimate(flops=cost, bytes_accessed=1 << 20, transcendentals=0),
    )(*scalars, *arrays)


def blur_rows_and_columns(depth, own, side, ly, bx, mid, out, flip):
    views, width = bx.shape[0], bx.shape[1] // 2
    window = own.rows + side.rows
    for z in range(0, depth, 2):
        pair = stack3(
            [jnp.concatenate([p.layer(z), p.layer(z + 1)], axis=1) for p in (own, side)]
        )
        result = dot(ly[...], pair)
        for v in range(views):
            for i in range(2):
                top, rest = parts(result[v * window : (v + 1) * window, i * width : (i + 1) * width])
                at = pl.ds((z + i) * window, window)
                mid[v, at, :width] = top
                mid[v, at, width:] = rest
    for v in range(views):
        for z in range(0, depth, 4):
            wide = dot(mid[v, pl.ds(z * window, 4 * window), :], bx[v])
            value = wide[:, :width] + wide[:, width:]
            for i in range(4):
                to = depth - 1 - z - i if flip else z + i
                out[v, to] = value[i * window : (i + 1) * window]


def ratios(seen, blurred):
    return [jnp.where(b > 0, d / b, 0.0) for d, b in zip(seen, blurred)]


def gather(total, at, term):
    total[at] = term if total[at] is None else total[at] + term


def near(depth, own, side, own_in, side_in, data_own, data_in, tables):
    taps, ly, bx = tables[:3]
    views, width = bx.shape[0], bx.shape[1] // 2
    window = own.rows + side.rows

    def body(_, pieces, blur_far, back, blur_own, blur_in, mid):
        own, side, own_in, side_in, taps, ly, bx = pieces[:7]
        taps, ly, bx = taps.array, ly.array, bx.array
        data_own, data_in = pieces[7 : 7 + views], pieces[7 + views :]
        blur_rows_and_columns(depth, own, side, ly, bx, mid, blur_own, False)
        blur_rows_and_columns(depth, own_in, side_in, ly, bx, mid, blur_in, True)
        for v in range(views):

            @pl.loop(0, window // R)
            def _(tile):
                y = pl.multiple_of(tile * R, R)
                at = pl.ds(y, R)
                load = lambda i: blur_own[v, i, at, :] if i < depth else blur_in[v, i - depth, at, :]
                blurred = [None] * depth
                for k in range(TAPS):
                    t = taps[v, k]
                    for j in range(depth):
                        gather(blurred, j, t * load(j + k))
                seen = [data_own[v].tile(j, y) for j in range(R)]
                seen += [data_in[v].tile(R - 1 - j, y) for j in range(R)]
                ratio = ratios(seen, blurred)
                total = [None] * depth
                for d in range(depth):
                    t = taps[v, d]
                    for j in range(depth - d):
                        gather(total, j + d, t * ratio[j])
                for z in range(depth):
                    back[v, z, at, :] = total[z]
                partial = [None] * depth
                for k in range(1, TAPS):
                    t = taps[v, k]
                    for j in range(depth - k, depth):
                        gather(partial, j, t * load(j + k - depth))
                for j in range(depth):
                    blur_far[v, j, at, :] = partial[j]

    shape = (views, depth, window, width)
    return call(
        body,
        [],
        [own, side, own_in, side_in] + [Piece(t, 0) for t in (taps, ly, bx)] + [*data_own, *data_in],
        [jax.ShapeDtypeStruct(shape, F32)] * 2,
        [pltpu.VMEM(shape, F32)] * 2 + [pltpu.VMEM((views, depth * window, 2 * width), BF16)],
        24 if views == 2 else 48,
        views * 10**9,
    )


def far(last, depth, scalars, est, own_out, side_out, blur_far, back, data_out, data_own, tables):
    views, width = tables[2].shape[0], tables[2].shape[1] // 2
    window, rows = own_out.rows + side_out.rows, est.rows

    def body(scalars, pieces, *refs):
        place, cover = scalars
        est, own_out, side_out = pieces[:3]
        blur_far, back, taps, ly, bx, lyt, bxt = [p.array for p in pieces[3:10]]
        data_out, data_own = pieces[10 : 10 + views], pieces[10 + views :]
        out, edge = refs[0], None if last else refs[1]
        blur_out, full, mid = refs[-3:]
        even = place[0] == 0
        blur_rows_and_columns(depth, own_out, side_out, ly, bx, mid, blur_out, True)
        for v in range(views):

            @pl.loop(0, window // R)
            def _(tile):
                y = pl.multiple_of(tile * R, R)
                at = pl.ds(y, R)
                blurred = [blur_far[v, j, at, :] for j in range(depth)]
                for k in range(depth):
                    t = taps[v, k]
                    for j in range(depth - k):
                        blurred[j] = blurred[j] + t * blur_out[v, j + k, at, :]
                seen = [data_out[v].tile(R - 1 - j, y) for j in range(R)]
                seen += [data_own[v].tile(j, y) for j in range(R)]
                ratio = ratios(seen, blurred)
                total = [back[v, z, at, :] for z in range(depth)]
                for d in range(depth):
                    t = taps[v, 2 * R - d]
                    for z in range(depth - d):
                        total[z] = total[z] + t * ratio[z + d]
                for z in range(depth):
                    full[v, z, at, :] = total[z]

        for z in range(0, depth, 2):
            for v in range(views):
                both = jnp.concatenate([full[v, z], full[v, z + 1]], axis=1)
                result = dot(lyt[v], stack3([both]))
                for i in range(2):
                    top, rest = parts(result[:, i * width : (i + 1) * width])
                    at = pl.ds((z + i) * rows, rows)
                    mid[v, at, :width] = top
                    mid[v, at, width:] = rest
        if views == 2:
            chosen = [cover[0, place[1]], cover[0, 1 - place[1]]]
        else:
            chosen = [cover[0, v] for v in range(views)]
        count = sum(chosen).astype(F32)
        for z in range(0, depth, 4):
            factor = None
            for v in range(views):
                wide = dot(mid[v, pl.ds(z * rows, 4 * rows), :], bxt[v])
                value = wide[:, :width] + wide[:, width:]
                if views == 2:
                    alone = chosen[1 - v] == 0
                    power = jnp.where(alone, value, jnp.sqrt(value))
                    power = jnp.where(chosen[v] == 0, 1.0, power)
                    factor = power if factor is None else factor * power
                else:
                    term = chosen[v].astype(F32) * jnp.log(value)
                    factor = term if factor is None else factor + term
            if views != 2:
                factor = jnp.exp(factor / count)
            for i in range(4):
                new = est.layer(z + i) * factor[i * rows : (i + 1) * rows]
                if last:
                    out[lax.select(even, jnp.int32(z + i), jnp.int32(depth - 1 - z - i))] = new
                else:
                    out[pl.ds((z + i) * rows, rows), :] = new
                    edge[pl.ds((z + i) * HALO, HALO), :] = jnp.where(
                        place[1] == 0, new[rows - HALO :], new[:HALO]
                    )

    shape = (views, depth, window, width)
    if last:
        outs = [jax.ShapeDtypeStruct((depth, rows, width), F32)]
    else:
        outs = [jax.ShapeDtypeStruct((depth * n, width), F32) for n in (rows, HALO)]
    return call(
        body,
        scalars,
        [est, own_out, side_out]
        + [Piece(t, 0) for t in (blur_far, back, *tables)]
        + [*data_out, *data_own],
        outs,
        [pltpu.VMEM(shape, F32)] * 2 + [pltpu.VMEM((views, depth * window, 2 * width), BF16)],
        24 if views == 2 else 48,
        views * 10**9,
    )


def normalized(taps):
    return taps / jnp.sum(taps, axis=-1, keepdims=True)


def small_rows(taps, first_shift, second_shift, width):
    lane = lax.broadcasted_iota(jnp.int32, (1, width), 1)
    shifts = jnp.where(lane == 0, first_shift.astype(F32), second_shift.astype(F32))
    return normalized(taps), shifts


def bands(place, smalls, rows, window, width):
    views, triple = len(smalls), 3 * window
    iota = lambda shape, dim: lax.broadcasted_iota(jnp.int32, shape, dim)

    def body(scalars, smalls, spread, ly, bx, lyt, bxt):
        (place,) = scalars
        low = place[2]

        def position(c):
            return jnp.where(c < rows, c, jnp.where(c < rows + low, c - rows - HALO, c - low))

        def split(value):
            top = value.astype(BF16).astype(F32)
            return top, value - top

        for v, piece in enumerate(smalls):
            small = piece.layer(0)

            def values(d, index):
                total = jnp.zeros(index.shape, F32)
                for k in range(TAPS):
                    total = jnp.where(index == k, small[d : d + 1, k : k + 1], total)
                return total

            shift = jnp.round(small[3:4, :]).astype(jnp.int32)
            for k in range(TAPS):
                there, back = small[0:1, k : k + 1], small[0:1, TAPS - 1 - k : TAPS - k]
                spread[v, k] = jnp.broadcast_to(jnp.where(place[0] == 0, there, back), (R, width))
            for out, height, mirror in ((ly, window, False), (lyt, rows, True)):
                col = iota((height, triple), 1)
                folded = position(
                    jnp.where(col < window, col, jnp.where(col < 2 * window, col - window, col - 2 * window))
                )
                line = position(iota((height, triple), 0))
                index = (line - folded if mirror else folded - line) + shift[:, 0:1] + R
                top, rest = split(values(1, index))
                both = jnp.where(col < 2 * window, top, rest).astype(BF16)
                if mirror:
                    out[v] = both
                else:
                    out[pl.ds(v * window, window), :] = both
            step = iota((width, width), 1) - iota((width, width), 0)
            for out, index in ((bx, -step), (bxt, step)):
                top, rest = split(values(2, index + shift[:, 1:2] + R))
                for i in range(2):
                    at = pl.ds(i * width, width)
                    out[v, at, :width] = top.astype(BF16)
                    out[v, at, width:] = rest.astype(BF16)

    shapes = [
        (views * window, triple),
        (views, 2 * width, 2 * width),
        (views, rows, triple),
        (views, 2 * width, 2 * width),
    ]
    return call(
        body,
        [place],
        smalls,
        [jax.ShapeDtypeStruct((views, TAPS, R, width), F32)]
        + [jax.ShapeDtypeStruct(s, BF16) for s in shapes],
        [],
        8,
        views * 10**8,
    )


def prepare(place, estimate, views_data, psf_taps, view_offsets):
    depth, rows, width = estimate.shape
    total = views_data.shape[2]
    window, half = rows + HALO, depth // 2

    def body(place, offsets, estimate, recorded, psf, outer, inner, across, corner, beside):
        mine, theirs = place[1], 1 - place[1]
        edge = pl.multiple_of(jnp.where(mine == 0, rows - HALO, 0), HALO)
        taps, shifts = small_rows(psf[0], offsets[0, 0], offsets[0, 1], width)
        small = depth * HALO + half * window
        across[pl.ds(small, R), :] = jnp.zeros((R, width), F32)
        across[pl.ds(small, 3), :TAPS] = taps
        across[pl.ds(small + 3, 1), :] = shifts

        def window_rows(view, at, out, to):
            start = pl.multiple_of(view * rows, R)
            out[pl.ds(to, rows), :] = recorded[0, at, pl.ds(start, rows), :]
            start = pl.multiple_of(jnp.where(view == 0, rows, total - rows - HALO), R)
            out[pl.ds(to + rows, HALO), :] = recorded[0, at, pl.ds(start, HALO), :]

        for z in range(depth):
            at = lax.select(place[0] == 0, jnp.int32(z), jnp.int32(depth - 1 - z))
            layer, strip = estimate[at], estimate[at, pl.ds(edge, HALO), :]
            for out in (outer, inner):
                out[pl.ds(z * rows, rows), :] = layer
            for out in (across, corner):
                out[pl.ds(z * HALO, HALO), :] = strip
            if z < half:
                window_rows(mine, at, outer, depth * rows + z * window)
                window_rows(theirs, at, corner, depth * HALO + z * window)
                window_rows(theirs, at, beside, z * window)
            else:
                window_rows(mine, at, inner, depth * rows + (z - half) * window)
                window_rows(theirs, at, across, depth * HALO + (z - half) * window)

    heights = [
        depth * rows + half * window,
        depth * rows + half * window,
        depth * HALO + half * window + R,
        depth * HALO + half * window,
        half * window,
    ]
    return pl.pallas_call(
        body,
        out_shape=[jax.ShapeDtypeStruct((height, width), F32) for height in heights],
        in_specs=[SMEM] * 2 + [VMEM] * 3,
        out_specs=[VMEM] * 5,
        compiler_params=pltpu.CompilerParams(vmem_limit_bytes=10 << 20),
        cost_estimate=pl.CostEstimate(flops=0, bytes_accessed=8 << 20, transcendentals=0),
        name="prepare",
    )(place, view_offsets, estimate, views_data, psf_taps)


def pair_lists(count):
    inner = [(i, i + 1) for i in range(0, count - 1, 2)]
    outer = [(i, i + 1) for i in range(1, count - 1, 2)]
    both = lambda pairs: [p for a, b in pairs for p in ((a, b), (b, a))]
    return both(inner), both(outer)


def diagonal(pairs):
    return [(2 * a + v, 2 * b + 1 - v) for a, b in pairs for v in range(2)]


def two_view_plan(estimate, views_data, psf_taps, view_offsets, place, inner, outer):
    swap = [(0, 1), (1, 0)]
    depth, rows, _ = estimate.shape
    window = rows + HALO
    both = ("brick", "view")
    wide, thin = depth * rows, depth * HALO
    small = thin + depth // 2 * window

    def halo(current, edge):
        if edge is None:
            return start
        outer_z = lax.ppermute(current.array, "brick", outer)
        side = lax.ppermute(edge, "view", swap)
        inner_z = lax.ppermute(current.array, "brick", inner)
        outer_side = lax.ppermute(edge, both, diagonal(outer))
        inner_side = lax.ppermute(side, "brick", inner)
        return (
            Piece(side, HALO), Piece(inner_z, rows), Piece(inner_side, HALO),
            Piece(outer_z, rows), Piece(outer_side, HALO),
        )

    to_outer, to_inner, across, corner, beside = prepare(
        place, estimate, views_data, psf_taps, view_offsets
    )
    from_outer = lax.ppermute(to_outer, "brick", outer)
    from_side = lax.ppermute(across, "view", swap)
    from_inner = lax.ppermute(to_inner, "brick", inner)
    from_corner = lax.ppermute(corner, both, diagonal(outer))
    from_beside = lax.ppermute(beside, "view", swap)
    from_inner_side = lax.ppermute(from_side, "brick", inner)
    start = (
        Piece(from_side, HALO), Piece(from_inner, rows), Piece(from_inner_side, HALO),
        Piece(from_outer, rows), Piece(from_corner, HALO),
    )
    near_data = (
        (Piece(to_inner, window, wide), Piece(from_side, window, thin)),
        (Piece(from_inner, window, wide), Piece(from_inner_side, window, thin)),
    )
    far_data = (
        (Piece(from_outer, window, wide), Piece(from_corner, window, thin)),
        (Piece(to_outer, window, wide), Piece(from_beside, window)),
    )
    smalls = (Piece(across, R, small), Piece(from_side, R, small))
    return Piece(to_inner, rows), smalls, near_data, far_data, halo, window


def many_view_plan(estimate, views_data, psf_taps, view_offsets, place, inner, outer):
    depth, rows, width = estimate.shape
    even = place[0] == 0
    up = [(i, i + 1) for i in range(lax.axis_size("view") - 1)]
    down = [(b, a) for a, b in up]
    flat = lambda array: Piece(array.reshape(-1, width), array.shape[1])

    def beside(block, dim):
        low = lax.slice_in_dim(block, rows - HALO, rows, axis=dim)
        high = lax.slice_in_dim(block, 0, HALO, axis=dim)
        return jnp.concatenate(
            [lax.ppermute(low, "view", up), lax.ppermute(high, "view", down)], axis=dim
        )

    def halo(current, _):
        block = current.array.reshape(depth, rows, width)
        inner_z = lax.ppermute(block, "brick", inner)
        outer_z = lax.ppermute(block, "brick", outer)
        pieces = beside(block, 1), inner_z, beside(inner_z, 1), outer_z, beside(outer_z, 1)
        return tuple(flat(piece) for piece in pieces)

    taps, shifts = small_rows(psf_taps[0], view_offsets[0, 0], view_offsets[0, 1], width)
    taps = jnp.pad(taps, ((0, 0), (0, width - TAPS)))
    small = jnp.concatenate([taps, shifts, jnp.zeros((R - 4, width), F32)])
    smalls = lax.all_gather(small, "view", axis=0, tiled=True)
    data = lax.all_to_all(views_data, "view", split_axis=2, concat_axis=0, tiled=True)
    data = jnp.where(even, data, data[:, ::-1])
    data = jnp.concatenate([data, beside(data, 2)], axis=2)
    views = range(data.shape[0])
    ends = lambda array: tuple(flat(array[v]) for v in views)
    mine_in, mine_out = data[:, -R:], data[:, :R]
    near_data = ends(mine_in), ends(lax.ppermute(mine_in, "brick", inner))
    far_data = ends(lax.ppermute(mine_out, "brick", outer)), ends(mine_out)
    current = flat(jnp.where(even, estimate, estimate[::-1]))
    smalls = tuple(Piece(smalls, R, v * R) for v in views)
    return current, smalls, near_data, far_data, halo, rows + 2 * HALO


def shards(estimate, views_data, psf_taps, view_offsets, coverage):
    brick, view = lax.axis_index("brick"), lax.axis_index("view")
    depth, rows, width = estimate.shape
    inner, outer = pair_lists(lax.axis_size("brick"))
    pair = lax.axis_size("view") == 2
    plan = two_view_plan if pair else many_view_plan
    low = jnp.where(view == 0, 0, HALO) if pair else HALO
    place = jnp.stack([lax.rem(brick, 2), view, low]).astype(jnp.int32)
    current, smalls, near_data, far_data, halo, window = plan(
        estimate, views_data, psf_taps, view_offsets, place, inner, outer
    )
    tables = bands(place, smalls, rows, window, width)
    edge = None
    for step in range(ITERS):
        last = step == ITERS - 1
        side, inner_z, inner_side, outer_z, outer_side = halo(current, edge)
        blur_far, back = near(
            depth, current, side, inner_z, inner_side, *near_data, tables
        )
        results = far(
            last, depth, [place, coverage], current, outer_z, outer_side,
            blur_far, back, *far_data, tables,
        )
        if not last:
            current, edge = Piece(results[0], rows), results[1]
    return results[0]


def solution(mesh):
    return jax.shard_map(
        shards,
        mesh=mesh,
        in_specs=(
            P("brick", "view", None),
            P("view", "brick", None, None),
            P("view", None, None),
            P("view", None),
            P("brick", None),
        ),
        out_specs=P("brick", "view", None),
        check_vma=False,
    )
```

```python
import jax
import jax.numpy as jnp
from jax import lax
from jax.experimental import pallas as pl
from jax.experimental.pallas import tpu as pltpu
from jax.sharding import PartitionSpec as P


R = 8
ITERS = 4
HALO = 2 * R

F32, BF16 = jnp.float32, jnp.bfloat16
VMEM = pl.BlockSpec(memory_space=pltpu.VMEM)
SMEM = pl.BlockSpec(memory_space=pltpu.SMEM)
TAPS = 2 * R + 1


def parts(x):
    top = x.astype(BF16)
    return top, (x - top.astype(F32)).astype(BF16)


def dot(a, b):
    return jnp.dot(a, b, preferred_element_type=F32)


def stack3(blocks):
    split = [parts(b) for b in blocks]
    tops, rests = [s[0] for s in split], [s[1] for s in split]
    return jnp.concatenate(tops + rests + tops, axis=0)


class Piece:
    def __init__(self, array, rows, start=0):
        self.array, self.rows, self.start = array, rows, start

    def on(self, ref):
        return Piece(ref, self.rows, self.start)

    def layer(self, z):
        return self.array[pl.ds(self.start + z * self.rows, self.rows), :]

    def tile(self, z, y):
        return self.array[pl.ds(pl.multiple_of(self.start + z * self.rows + y, R), R), :]


def call(body, scalars, pieces, out_shape, scratch, vmem, cost):
    arrays = []
    for piece in pieces:
        if not any(piece.array is array for array in arrays):
            arrays.append(piece.array)
    where = [next(i for i, array in enumerate(arrays) if array is p.array) for p in pieces]

    def kernel(*refs):
        inputs = refs[len(scalars) : len(scalars) + len(arrays)]
        body(
            refs[: len(scalars)],
            [p.on(inputs[i]) for p, i in zip(pieces, where)],
            *refs[len(scalars) + len(arrays) :],
        )

    return pl.pallas_call(
        kernel,
        out_shape=out_shape,
        in_specs=[SMEM] * len(scalars) + [VMEM] * len(arrays),
        out_specs=[VMEM] * len(out_shape),
        scratch_shapes=scratch,
        compiler_params=pltpu.CompilerParams(vmem_limit_bytes=vmem << 20),
        cost_estimate=pl.CostEstimate(flops=cost, bytes_accessed=1 << 20, transcendentals=0),
    )(*scalars, *arrays)


def blur_rows_and_columns(depth, own, side, ly, bx, mid, out, flip):
    views, width = bx.shape[0], bx.shape[1] // 2
    window = own.rows + side.rows
    for z in range(0, depth, 2):
        pair = stack3(
            [jnp.concatenate([p.layer(z), p.layer(z + 1)], axis=1) for p in (own, side)]
        )
        result = dot(ly[...], pair)
        for v in range(views):
            for i in range(2):
                top, rest = parts(result[v * window : (v + 1) * window, i * width : (i + 1) * width])
                at = pl.ds((z + i) * window, window)
                mid[v, at, :width] = top
                mid[v, at, width:] = rest
    for v in range(views):
        for z in range(0, depth, 4):
            wide = dot(mid[v, pl.ds(z * window, 4 * window), :], bx[v])
            value = wide[:, :width] + wide[:, width:]
            for i in range(4):
                to = depth - 1 - z - i if flip else z + i
                out[v, to] = value[i * window : (i + 1) * window]


def ratios(seen, blurred):
    return [jnp.where(b > 0, d * pl.reciprocal(b), 0.0) for d, b in zip(seen, blurred)]


def gather(total, at, term):
    total[at] = term if total[at] is None else total[at] + term


def near(depth, own, side, own_in, side_in, data_own, data_in, tables):
    taps, ly, bx = tables[:3]
    views, width = bx.shape[0], bx.shape[1] // 2
    window = own.rows + side.rows

    def body(_, pieces, blur_far, back, blur_own, blur_in, mid):
        own, side, own_in, side_in, taps, ly, bx = pieces[:7]
        taps, ly, bx = taps.array, ly.array, bx.array
        data_own, data_in = pieces[7 : 7 + views], pieces[7 + views :]
        blur_rows_and_columns(depth, own, side, ly, bx, mid, blur_own, False)
        blur_rows_and_columns(depth, own_in, side_in, ly, bx, mid, blur_in, True)
        for v in range(views):

            @pl.loop(0, window // R)
            def _(tile):
                y = pl.multiple_of(tile * R, R)
                at = pl.ds(y, R)
                load = lambda i: blur_own[v, i, at, :] if i < depth else blur_in[v, i - depth, at, :]
                blurred = [None] * depth
                for k in range(TAPS):
                    t = taps[v, k]
                    for j in range(depth):
                        gather(blurred, j, t * load(j + k))
                seen = [data_own[v].tile(j, y) for j in range(R)]
                seen += [data_in[v].tile(R - 1 - j, y) for j in range(R)]
                ratio = ratios(seen, blurred)
                total = [None] * depth
                for d in range(depth):
                    t = taps[v, d]
                    for j in range(depth - d):
                        gather(total, j + d, t * ratio[j])
                for z in range(depth):
                    back[v, z, at, :] = total[z]
                partial = [None] * depth
                for k in range(1, TAPS):
                    t = taps[v, k]
                    for j in range(depth - k, depth):
                        gather(partial, j, t * load(j + k - depth))
                for j in range(depth):
                    blur_far[v, j, at, :] = partial[j]

    shape = (views, depth, window, width)
    return call(
        body,
        [],
        [own, side, own_in, side_in] + [Piece(t, 0) for t in (taps, ly, bx)] + [*data_own, *data_in],
        [jax.ShapeDtypeStruct(shape, F32)] * 2,
        [pltpu.VMEM(shape, F32)] * 2 + [pltpu.VMEM((views, depth * window, 2 * width), BF16)],
        24 if views == 2 else 48,
        views * 10**9,
    )


def far(last, depth, scalars, est, own_out, side_out, blur_far, back, data_out, data_own, tables):
    views, width = tables[2].shape[0], tables[2].shape[1] // 2
    window, rows = own_out.rows + side_out.rows, est.rows

    def body(scalars, pieces, *refs):
        place, cover = scalars
        est, own_out, side_out = pieces[:3]
        blur_far, back, taps, ly, bx, lyt, bxt = [p.array for p in pieces[3:10]]
        data_out, data_own = pieces[10 : 10 + views], pieces[10 + views :]
        out, edge = refs[0], None if last else refs[1]
        blur_out, full, mid = refs[-3:]
        even = place[0] == 0
        blur_rows_and_columns(depth, own_out, side_out, ly, bx, mid, blur_out, True)
        for v in range(views):

            @pl.loop(0, window // R)
            def _(tile):
                y = pl.multiple_of(tile * R, R)
                at = pl.ds(y, R)
                blurred = [blur_far[v, j, at, :] for j in range(depth)]
                for k in range(depth):
                    t = taps[v, k]
                    for j in range(depth - k):
                        blurred[j] = blurred[j] + t * blur_out[v, j + k, at, :]
                seen = [data_out[v].tile(R - 1 - j, y) for j in range(R)]
                seen += [data_own[v].tile(j, y) for j in range(R)]
                ratio = ratios(seen, blurred)
                total = [back[v, z, at, :] for z in range(depth)]
                for d in range(depth):
                    t = taps[v, 2 * R - d]
                    for z in range(depth - d):
                        total[z] = total[z] + t * ratio[z + d]
                for z in range(depth):
                    full[v, z, at, :] = total[z]

        for z in range(0, depth, 2):
            for v in range(views):
                both = jnp.concatenate([full[v, z], full[v, z + 1]], axis=1)
                result = dot(lyt[v], stack3([both]))
                for i in range(2):
                    top, rest = parts(result[:, i * width : (i + 1) * width])
                    at = pl.ds((z + i) * rows, rows)
                    mid[v, at, :width] = top
                    mid[v, at, width:] = rest
        if views == 2:
            chosen = [cover[0, place[1]], cover[0, 1 - place[1]]]
        else:
            chosen = [cover[0, v] for v in range(views)]
        count = sum(chosen).astype(F32)
        for z in range(0, depth, 4):
            factor = None
            for v in range(views):
                wide = dot(mid[v, pl.ds(z * rows, 4 * rows), :], bxt[v])
                value = wide[:, :width] + wide[:, width:]
                if views == 2:
                    alone = chosen[1 - v] == 0
                    root = jnp.where(value > 0, value * lax.rsqrt(value), value)
                    power = jnp.where(alone, value, root)
                    power = jnp.where(chosen[v] == 0, 1.0, power)
                    factor = power if factor is None else factor * power
                else:
                    term = chosen[v].astype(F32) * jnp.log(value)
                    factor = term if factor is None else factor + term
            if views != 2:
                factor = jnp.exp(factor / count)
            for i in range(4):
                new = est.layer(z + i) * factor[i * rows : (i + 1) * rows]
                if last:
                    out[lax.select(even, jnp.int32(z + i), jnp.int32(depth - 1 - z - i))] = new
                else:
                    out[pl.ds((z + i) * rows, rows), :] = new
                    edge[pl.ds((z + i) * HALO, HALO), :] = jnp.where(
                        place[1] == 0, new[rows - HALO :], new[:HALO]
                    )

    shape = (views, depth, window, width)
    if last:
        outs = [jax.ShapeDtypeStruct((depth, rows, width), F32)]
    else:
        outs = [jax.ShapeDtypeStruct((depth * n, width), F32) for n in (rows, HALO)]
    return call(
        body,
        scalars,
        [est, own_out, side_out]
        + [Piece(t, 0) for t in (blur_far, back, *tables)]
        + [*data_out, *data_own],
        outs,
        [pltpu.VMEM(shape, F32)] * 2 + [pltpu.VMEM((views, depth * window, 2 * width), BF16)],
        24 if views == 2 else 48,
        views * 10**9,
    )


def normalized(taps):
    return taps / jnp.sum(taps, axis=-1, keepdims=True)


def small_rows(taps, first_shift, second_shift, width):
    lane = lax.broadcasted_iota(jnp.int32, (1, width), 1)
    shifts = jnp.where(lane == 0, first_shift.astype(F32), second_shift.astype(F32))
    return normalized(taps), shifts


def bands(place, smalls, rows, window, width):
    views, triple = len(smalls), 3 * window
    iota = lambda shape, dim: lax.broadcasted_iota(jnp.int32, shape, dim)

    def body(scalars, smalls, spread, ly, bx, lyt, bxt):
        (place,) = scalars
        low = place[2]

        def position(c):
            return jnp.where(c < rows, c, jnp.where(c < rows + low, c - rows - HALO, c - low))

        def split(value):
            top = value.astype(BF16).astype(F32)
            return top, value - top

        for v, piece in enumerate(smalls):
            small = piece.layer(0)

            def values(d, index):
                total = jnp.zeros(index.shape, F32)
                for k in range(TAPS):
                    total = jnp.where(index == k, small[d : d + 1, k : k + 1], total)
                return total

            shift = jnp.round(small[3:4, :]).astype(jnp.int32)
            for k in range(TAPS):
                there, back = small[0:1, k : k + 1], small[0:1, TAPS - 1 - k : TAPS - k]
                spread[v, k] = jnp.broadcast_to(jnp.where(place[0] == 0, there, back), (R, width))
            for out, height, mirror in ((ly, window, False), (lyt, rows, True)):
                col = iota((height, triple), 1)
                folded = position(
                    jnp.where(col < window, col, jnp.where(col < 2 * window, col - window, col - 2 * window))
                )
                line = position(iota((height, triple), 0))
                index = (line - folded if mirror else folded - line) + shift[:, 0:1] + R
                top, rest = split(values(1, index))
                both = jnp.where(col < 2 * window, top, rest).astype(BF16)
                if mirror:
                    out[v] = both
                else:
                    out[pl.ds(v * window, window), :] = both
            step = iota((width, width), 1) - iota((width, width), 0)
            for out, index in ((bx, -step), (bxt, step)):
                top, rest = split(values(2, index + shift[:, 1:2] + R))
                for i in range(2):
                    at = pl.ds(i * width, width)
                    out[v, at, :width] = top.astype(BF16)
                    out[v, at, width:] = rest.astype(BF16)

    shapes = [
        (views * window, triple),
        (views, 2 * width, 2 * width),
        (views, rows, triple),
        (views, 2 * width, 2 * width),
    ]
    return call(
        body,
        [place],
        smalls,
        [jax.ShapeDtypeStruct((views, TAPS, R, width), F32)]
        + [jax.ShapeDtypeStruct(s, BF16) for s in shapes],
        [],
        8,
        views * 10**8,
    )


def prepare(place, estimate, views_data, psf_taps, view_offsets):
    depth, rows, width = estimate.shape
    total = views_data.shape[2]
    window, half = rows + HALO, depth // 2

    def body(place, estimate, recorded, psf, outer, inner, across, corner, beside):
        mine, theirs = place[1], 1 - place[1]
        edge = pl.multiple_of(jnp.where(mine == 0, rows - HALO, 0), HALO)
        taps, shifts = small_rows(psf[0], place[3], place[4], width)
        small = depth * HALO + half * window
        across[pl.ds(small, R), :] = jnp.zeros((R, width), F32)
        across[pl.ds(small, 3), :TAPS] = taps
        across[pl.ds(small + 3, 1), :] = shifts

        def window_rows(view, at, out, to):
            start = pl.multiple_of(view * rows, R)
            out[pl.ds(to, rows), :] = recorded[0, at, pl.ds(start, rows), :]
            start = pl.multiple_of(jnp.where(view == 0, rows, total - rows - HALO), R)
            out[pl.ds(to + rows, HALO), :] = recorded[0, at, pl.ds(start, HALO), :]

        for z in range(depth):
            at = lax.select(place[0] == 0, jnp.int32(z), jnp.int32(depth - 1 - z))
            layer, strip = estimate[at], estimate[at, pl.ds(edge, HALO), :]
            for out in (outer, inner):
                out[pl.ds(z * rows, rows), :] = layer
            for out in (across, corner):
                out[pl.ds(z * HALO, HALO), :] = strip
            if z < half:
                window_rows(mine, at, outer, depth * rows + z * window)
                window_rows(theirs, at, corner, depth * HALO + z * window)
                window_rows(theirs, at, beside, z * window)
            else:
                window_rows(mine, at, inner, depth * rows + (z - half) * window)
                window_rows(theirs, at, across, depth * HALO + (z - half) * window)

    heights = [
        depth * rows + half * window,
        depth * rows + half * window,
        depth * HALO + half * window + R,
        depth * HALO + half * window,
        half * window,
    ]
    return pl.pallas_call(
        body,
        out_shape=[jax.ShapeDtypeStruct((height, width), F32) for height in heights],
        in_specs=[SMEM] + [VMEM] * 3,
        out_specs=[VMEM] * 5,
        compiler_params=pltpu.CompilerParams(vmem_limit_bytes=10 << 20),
        cost_estimate=pl.CostEstimate(flops=0, bytes_accessed=8 << 20, transcendentals=0),
        name="prepare",
    )(jnp.concatenate([place, view_offsets[0]]), estimate, views_data, psf_taps)


def pair_lists(count):
    inner = [(i, i + 1) for i in range(0, count - 1, 2)]
    outer = [(i, i + 1) for i in range(1, count - 1, 2)]
    both = lambda pairs: [p for a, b in pairs for p in ((a, b), (b, a))]
    return both(inner), both(outer)


def diagonal(pairs):
    return [(2 * a + v, 2 * b + 1 - v) for a, b in pairs for v in range(2)]


def two_view_plan(estimate, views_data, psf_taps, view_offsets, place, inner, outer):
    swap = [(0, 1), (1, 0)]
    depth, rows, _ = estimate.shape
    window = rows + HALO
    both = ("brick", "view")
    wide, thin = depth * rows, depth * HALO
    small = thin + depth // 2 * window

    def halo(current, edge):
        if edge is None:
            return start
        outer_z = lax.ppermute(current.array, "brick", outer)
        side = lax.ppermute(edge, "view", swap)
        inner_z = lax.ppermute(current.array, "brick", inner)
        outer_side = lax.ppermute(edge, both, diagonal(outer))
        inner_side = lax.ppermute(side, "brick", inner)
        return (
            Piece(side, HALO), Piece(inner_z, rows), Piece(inner_side, HALO),
            Piece(outer_z, rows), Piece(outer_side, HALO),
        )

    to_outer, to_inner, across, corner, beside = prepare(
        place, estimate, views_data, psf_taps, view_offsets
    )
    from_outer = lax.ppermute(to_outer, "brick", outer)
    from_side = lax.ppermute(across, "view", swap)
    from_inner = lax.ppermute(to_inner, "brick", inner)
    from_corner = lax.ppermute(corner, both, diagonal(outer))
    from_beside = lax.ppermute(beside, "view", swap)
    from_inner_side = lax.ppermute(from_side, "brick", inner)
    start = (
        Piece(from_side, HALO), Piece(from_inner, rows), Piece(from_inner_side, HALO),
        Piece(from_outer, rows), Piece(from_corner, HALO),
    )
    near_data = (
        (Piece(to_inner, window, wide), Piece(from_side, window, thin)),
        (Piece(from_inner, window, wide), Piece(from_inner_side, window, thin)),
    )
    far_data = (
        (Piece(from_outer, window, wide), Piece(from_corner, window, thin)),
        (Piece(to_outer, window, wide), Piece(from_beside, window)),
    )
    smalls = (Piece(across, R, small), Piece(from_side, R, small))
    return Piece(to_inner, rows), smalls, near_data, far_data, halo, window


def many_view_plan(estimate, views_data, psf_taps, view_offsets, place, inner, outer):
    depth, rows, width = estimate.shape
    even = place[0] == 0
    up = [(i, i + 1) for i in range(lax.axis_size("view") - 1)]
    down = [(b, a) for a, b in up]
    flat = lambda array: Piece(array.reshape(-1, width), array.shape[1])

    def beside(block, dim):
        low = lax.slice_in_dim(block, rows - HALO, rows, axis=dim)
        high = lax.slice_in_dim(block, 0, HALO, axis=dim)
        return jnp.concatenate(
            [lax.ppermute(low, "view", up), lax.ppermute(high, "view", down)], axis=dim
        )

    def halo(current, _):
        block = current.array.reshape(depth, rows, width)
        inner_z = lax.ppermute(block, "brick", inner)
        outer_z = lax.ppermute(block, "brick", outer)
        pieces = beside(block, 1), inner_z, beside(inner_z, 1), outer_z, beside(outer_z, 1)
        return tuple(flat(piece) for piece in pieces)

    taps, shifts = small_rows(psf_taps[0], view_offsets[0, 0], view_offsets[0, 1], width)
    taps = jnp.pad(taps, ((0, 0), (0, width - TAPS)))
    small = jnp.concatenate([taps, shifts, jnp.zeros((R - 4, width), F32)])
    smalls = lax.all_gather(small, "view", axis=0, tiled=True)
    data = lax.all_to_all(views_data, "view", split_axis=2, concat_axis=0, tiled=True)
    data = jnp.where(even, data, data[:, ::-1])
    data = jnp.concatenate([data, beside(data, 2)], axis=2)
    views = range(data.shape[0])
    ends = lambda array: tuple(flat(array[v]) for v in views)
    mine_in, mine_out = data[:, -R:], data[:, :R]
    near_data = ends(mine_in), ends(lax.ppermute(mine_in, "brick", inner))
    far_data = ends(lax.ppermute(mine_out, "brick", outer)), ends(mine_out)
    current = flat(jnp.where(even, estimate, estimate[::-1]))
    smalls = tuple(Piece(smalls, R, v * R) for v in views)
    return current, smalls, near_data, far_data, halo, rows + 2 * HALO


def shards(estimate, views_data, psf_taps, view_offsets, coverage):
    brick, view = lax.axis_index("brick"), lax.axis_index("view")
    depth, rows, width = estimate.shape
    inner, outer = pair_lists(lax.axis_size("brick"))
    pair = lax.axis_size("view") == 2
    plan = two_view_plan if pair else many_view_plan
    low = jnp.where(view == 0, 0, HALO) if pair else HALO
    place = jnp.stack([lax.rem(brick, 2), view, low]).astype(jnp.int32)
    current, smalls, near_data, far_data, halo, window = plan(
        estimate, views_data, psf_taps, view_offsets, place, inner, outer
    )
    tables = bands(place, smalls, rows, window, width)
    edge = None
    for step in range(ITERS):
        last = step == ITERS - 1
        side, inner_z, inner_side, outer_z, outer_side = halo(current, edge)
        blur_far, back = near(
            depth, current, side, inner_z, inner_side, *near_data, tables
        )
        results = far(
            last, depth, [place, coverage], current, outer_z, outer_side,
            blur_far, back, *far_data, tables,
        )
        if not last:
            current, edge = Piece(results[0], rows), results[1]
    return results[0]


def solution(mesh):
    return jax.shard_map(
        shards,
        mesh=mesh,
        in_specs=(
            P("brick", "view", None),
            P("view", "brick", None, None),
            P("view", None, None),
            P("view", None),
            P("brick", None),
        ),
        out_specs=P("brick", "view", None),
        check_vma=False,
    )
```
